256 devices in a mesh: dp: 4 (over z_lo), space: 64 (over z_hi, x, y, core).
Axes of the slice: x: 4, y: 4, z: 8 (z_hi: 2, z_lo: 4; z = z_hi * 4 + z_lo), core: 2. Of those that a mesh axis runs over, the one named last changes fastest.
Arguments:
- volumes: bfloat16 [4, 64, 2, 8, 16, 256], P('dp', 'space'), may hold values from -6 to 6
- weight: bfloat16 [256, 6912], P('space', 'dp'), may hold values from -0.078125 to 0.078125
- cotangent: bfloat16 [4, 64, 2, 8, 16, 256], P('dp', 'space'), may hold values from -6 to 6
Outputs:
- features: bfloat16 [4, 64, 2, 8, 16, 256], P('dp', 'space')
- input_grad: bfloat16 [4, 64, 2, 8, 16, 256], P('dp', 'space')
- weight_grad: float32 [256, 6912], P('space', 'dp')
The draws below stay inside these ranges and needn't reach their ends.
All inputs are finite; a program needn't handle non-finite values.
Results may differ from the reference program's by a relative error of at most 0.0034.
Values may be sent and summed in bfloat16 or wider, within the bound.
No kernel may reach another device: no remote copies, remote signals or barrier semaphores. Data moves between devices by JAX's collectives and lax.ppermute only.
A program may use at most 128 MiB of HBM per device.

```python
import math
import jax
import jax.numpy as jnp
import numpy as np
from jax import lax

C = 256
CX = 2
CY = 8
NZ = 16
GY = 8
GX = 8
VOLUMES = 4
NX = 16
NY = 64
VOXELS = 65536
N_SPACE = 64


def block_levels(own_key, dims, pieces, least, largest):
    factor_of = 1.0
    for position, blocks in pieces:
        steps = jax.random.uniform(jax.random.fold_in(jax.random.fold_in(own_key, 6), position), (blocks,), jnp.float32, least / len(pieces), largest / len(pieces))
        factor_of = factor_of * jnp.repeat(jnp.exp(steps), dims[position] // blocks).reshape((-1,) + (1,) * (len(dims) - 1 - position))
    return factor_of


def centred(own_key, dims, spread, bound, pieces=(), dtype=jnp.bfloat16):
    factor_of = block_levels(own_key, dims, pieces, -0.22, 0.18) if pieces else 1.0
    drawn = jax.random.normal(own_key, dims, jnp.float32) * spread * factor_of
    return jnp.minimum(jnp.maximum(drawn, -bound), bound).astype(dtype)


def setup_inputs(seed: int = 0) -> dict:
    key_of = jax.random.split(jax.random.key(seed), 4)
    return {
        "volumes": centred(key_of[0], (VOLUMES, N_SPACE, CX, CY, NZ, C), 1.0, 6.0, ((0, 4), (1, 64))),
        "weight": centred(key_of[1], (C, 27 * C), (27 * C) ** -0.5, 0.078125, ((0, 64), (1, 4))),
        "cotangent": centred(key_of[2], (VOLUMES, N_SPACE, CX, CY, NZ, C), 1.0, 6.0, ((0, 4), (1, 64))),
    }


def border_tables():
    rows = np.arange(NX + 2)[:, None] - 1
    cols = np.arange(NY + 2)[None, :] - 1
    shifted = rows + CX * ((cols >= NY).astype(np.int64) - (cols < 0).astype(np.int64))
    first = np.mod(shifted, NX) + 0 * cols
    second = np.mod(cols, NY) + 0 * rows
    return (first.astype(np.int32), second.astype(np.int32))

def convolve(field, kernel):
    first, second = border_tables()
    padded = field[:, jnp.asarray(first), jnp.asarray(second)]
    return lax.conv_general_dilated(padded, kernel, (1, 1, 1), ((0, 0), (0, 0), (1, 1)), dimension_numbers=('NDHWC', 'DHWIO', 'NDHWC'), precision=lax.Precision.HIGHEST)

def assemble(blocks):
    shaped = blocks.reshape(VOLUMES, GX, GY, CX, CY, NZ, C).transpose(0, 1, 3, 2, 4, 5, 6)
    return shaped.reshape(VOLUMES, NX, NY, NZ, C)

def split_blocks(whole):
    shaped = whole.reshape(VOLUMES, GX, CX, GY, CY, NZ, C).transpose(0, 1, 3, 2, 4, 5, 6)
    return shaped.reshape(VOLUMES, N_SPACE, CX, CY, NZ, C)

def reference(volumes, weight, cotangent):
    kernel = weight.astype(jnp.float32).reshape(C, 3, 3, 3, C).transpose(1, 2, 3, 4, 0)
    inputs = assemble(volumes).astype(jnp.float32)
    grads = assemble(cotangent).astype(jnp.float32)
    output, pullback = jax.vjp(convolve, inputs, kernel)
    input_grad, kernel_grad = pullback(grads)
    weight_grad = kernel_grad.transpose(4, 0, 1, 2, 3).reshape(C, 27 * C) / math.sqrt(VOXELS)
    features = split_blocks(output.astype(jnp.bfloat16))
    return (features, split_blocks(input_grad.astype(jnp.bfloat16)), weight_grad)
```

```python
import functools
import math

import jax
import jax.numpy as jnp
from jax import lax
from jax.experimental import pallas as pl
from jax.experimental.pallas import tpu as pltpu
from jax.sharding import Mesh
from jax.sharding import PartitionSpec as P


F32 = jnp.float32
BF16 = jnp.bfloat16
C = 256
GROUPS_A = 5
COLS_A = GROUPS_A * 3 * C
SPACE = ("zh", "x", "y", "c")


def ring_get(block, axis, rel):
    n = lax.axis_size(axis)
    return lax.ppermute(block, axis, [((i + rel) % n, i) for i in range(n)])


def ring_put(block, axis, rel):
    n = lax.axis_size(axis)
    return lax.ppermute(block, axis, [(i, (i + rel) % n) for i in range(n)])


def swap_core(block):
    return lax.ppermute(block, "c", [(0, 1), (1, 0)])


def halo(stacked):
    x = lax.axis_index("x")
    side = lax.axis_index("y") * 2 + lax.axis_index("c")
    rows = ("zh", "x")
    first, last = stacked[:, :1], stacked[:, -1:]
    near = [(g, g + 1) for g in range(8) if g % 4 != 3]
    far = [(3, 4), (7, 0), (4, 3), (0, 7)]
    wrapped = lax.ppermute(jnp.where(x == 3, last, first), rows, far)
    lower = lax.ppermute(last, rows, near)
    upper = lax.ppermute(first, rows, [(b, a) for a, b in near])
    lower = jnp.where(x == 0, wrapped, lower)
    upper = jnp.where(x == 3, wrapped, upper)
    ext = jnp.concatenate((lower, stacked, upper), axis=1)
    first, last = ext[:, :, :1], ext[:, :, -1:]
    near = [(h, h + 1) for h in range(7)]
    far = [(8 * g + 7, (8 * g + 8) % 64) for g in range(8)]
    far = far + [(b, a) for a, b in far]
    wrapped = lax.ppermute(jnp.where(side == 7, last, first), SPACE, far)
    lower = lax.ppermute(last, ("y", "c"), near)
    upper = lax.ppermute(first, ("y", "c"), [(b, a) for a, b in near])
    lower = jnp.where(side == 0, wrapped, lower)
    upper = jnp.where(side == 7, wrapped, upper)
    return jnp.concatenate((lower, ext, upper), axis=2)


def row_map(x_major):
    n = jnp.arange(C, dtype=jnp.int32)
    core, outer, inner, zh, r = n // 128, n // 32 % 4, n // 8 % 4, n // 4 % 2, n % 4
    dx, dy = (outer, inner) if x_major else (inner, outer)
    gx = (lax.axis_index("x") + dx) % 4
    gy = (lax.axis_index("y") + dy) % 4
    gc = (lax.axis_index("c") + core) % 2
    return zh * 128 + gx * 32 + gy * 8 + gc * 4 + r


def one_hot(rows):
    n = jnp.arange(C, dtype=jnp.int32)
    return (rows[:, None] == n[None, :]).astype(BF16)


def one_hot_t(rows):
    n = jnp.arange(C, dtype=jnp.int32)
    return (n[:, None] == rows[None, :]).astype(BF16)


def fill_shifts(src, dst):
    wide = src[...].astype(F32)
    k = lax.broadcasted_iota(jnp.int32, wide.shape, 0) % 16
    n = wide.shape[0]
    dst[0] = jnp.where(k == 0, 0.0, pltpu.roll(wide, 1, 0)).astype(BF16)
    dst[1] = src[...]
    dst[2] = jnp.where(k == 15, 0.0, pltpu.roll(wide, n - 1, 0)).astype(BF16)


def tap_rows(shifts, a, b, c):
    lo = a * 160 + b * 16
    return jnp.concatenate((shifts[c, lo : lo + 128], shifts[c, lo + 160 : lo + 288]), axis=0)


NT = (((1,), (1,)), ((), ()))


def wgrad_kernel(groups, vol, cot, perm, keep, send, shifts):
    fill_shifts(vol, shifts)
    cot_t = lax.dot_general(perm[...], cot[...], NT, preferred_element_type=F32).astype(BF16)
    for n, g in enumerate(groups):
        for c in range(3):
            rows = tap_rows(shifts, g // 3, g % 3, c)
            out = jnp.dot(cot_t, rows, preferred_element_type=F32)
            lo = (3 * n + c) * C
            keep[:, lo : lo + C] = out[:128]
            send[:, lo : lo + C] = out[128:].astype(BF16)


def wgrad(vol, cot, perm, groups):
    cols = len(groups) * 3 * C
    return pl.pallas_call(
        functools.partial(wgrad_kernel, groups),
        out_shape=(
            jax.ShapeDtypeStruct((128, cols), F32),
            jax.ShapeDtypeStruct((128, cols), BF16),
        ),
        scratch_shapes=[pltpu.VMEM((3, 640, C), BF16)],
        compiler_params=pltpu.CompilerParams(vmem_limit_bytes=40 << 20),
    )(vol, cot, perm)


def conv_kernel(vol, cot, wa0, wa1, wb0, wb1, qa, qb, feat, grad, vs, cs):
    fill_shifts(vol, vs)
    fill_shifts(cot, cs)
    acc_f = jnp.zeros((C, C), F32)
    acc_g = jnp.zeros((C, C), F32)
    for g in range(9):
        a, b = g // 3, g % 3
        own, other, q = (wa0, wa1, qa) if g < GROUPS_A else (wb0, wb1, qb)
        lo = (g if g < GROUPS_A else g - GROUPS_A) * 3 * C
        w = jnp.concatenate((own[:, lo : lo + 3 * C], other[:, lo : lo + 3 * C]), axis=0)
        w = jnp.dot(q[...], w, preferred_element_type=F32).astype(BF16)
        v = jnp.concatenate([tap_rows(vs, a, b, c) for c in range(3)], axis=1)
        acc_f += lax.dot_general(v, w, NT, preferred_element_type=F32)
        for c in range(3):
            rows = tap_rows(cs, 2 - a, 2 - b, 2 - c)
            acc_g += jnp.dot(rows, w[:, c * C : c * C + C], preferred_element_type=F32)
    feat[...] = acc_f.astype(BF16)
    grad[...] = acc_g.astype(BF16)


def conv(vol, cot, wa0, wa1, wb0, wb1, qa, qb):
    out = jax.ShapeDtypeStruct((C, C), BF16)
    return pl.pallas_call(
        conv_kernel,
        out_shape=(out, out),
        scratch_shapes=[pltpu.VMEM((3, 640, C), BF16), pltpu.VMEM((3, 640, C), BF16)],
        compiler_params=pltpu.CompilerParams(vmem_limit_bytes=40 << 20),
    )(vol, cot, wa0, wa1, wb0, wb1, qa, qb)


def gather_stage(block, axis):
    return jnp.concatenate([block] + [ring_get(block, axis, rel) for rel in (1, 2, 3)], axis=0)


def scatter_stage(block, axis):
    n = block.shape[0] // 4
    out = block[:n]
    for rel in (1, 2, 3):
        part = block[rel * n : rel * n + n].astype(BF16)
        out = out + ring_put(part, axis, rel).astype(F32)
    return out


def per_device(volumes, weight, cotangent):
    own_cot = cotangent.reshape(C, C)
    ext = halo(jnp.stack((volumes[0, 0], cotangent[0, 0])))
    vol = ext[0].reshape(640, C)
    cot = ext[1].reshape(640, C)

    rows, cols = weight.shape
    spread = jnp.broadcast_to(weight, (8, rows, cols))
    along_z = lax.all_to_all(spread, ("dp", "zh"), 0, 0, tiled=True)
    wz = along_z.reshape(4, 2, rows, cols).transpose(1, 2, 0, 3).reshape(8, 4 * cols)
    wa = gather_stage(gather_stage(wz[:, :COLS_A], "x"), "y")
    wb = gather_stage(gather_stage(wz[:, COLS_A:], "y"), "x")
    wa1 = swap_core(wa)
    wb1 = swap_core(wb)

    map_x, map_y = row_map(True), row_map(False)
    keep_a, send_a = wgrad(vol, own_cot, one_hot(map_x), tuple(range(GROUPS_A)))
    keep_b, send_b = wgrad(vol, own_cot, one_hot(map_y), tuple(range(GROUPS_A, 9)))
    sum_a = keep_a + swap_core(send_a).astype(F32)
    sum_b = keep_b + swap_core(send_b).astype(F32)
    sum_a = scatter_stage(scatter_stage(sum_a, "x"), "y")
    sum_b = scatter_stage(scatter_stage(sum_b, "y"), "x")
    part = jnp.concatenate((sum_a, sum_b), axis=1)
    part = part.reshape(2, rows, 4, cols).transpose(2, 0, 1, 3).reshape(8, rows, cols)
    part = lax.all_to_all(part, ("dp", "zh"), 0, 0, tiled=True)
    factor = 1.0 / math.sqrt(C * 256)
    weight_grad = jnp.sum(part, axis=0) * factor

    features, input_grad = conv(vol, cot, wa, wa1, wb, wb1, one_hot_t(map_y), one_hot_t(map_x))
    return (features.reshape(volumes.shape), input_grad.reshape(volumes.shape), weight_grad)


def solution(mesh):
    fine = Mesh(mesh.devices.reshape(4, 2, 4, 4, 2), ("dp",) + SPACE)
    blocks = P("dp", SPACE, None, None, None, None)
    return jax.shard_map(
        per_device,
        mesh=fine,
        in_specs=(blocks, P(SPACE, "dp"), blocks),
        out_specs=(blocks, blocks, P(SPACE, "dp")),
        check_vma=False,
    )
```

```python
import functools
import math

import jax
import jax.numpy as jnp
from jax import lax
from jax.experimental import pallas as pl
from jax.experimental.pallas import tpu as pltpu
from jax.sharding import Mesh
from jax.sharding import PartitionSpec as P


F32 = jnp.float32
BF16 = jnp.bfloat16
C = 256
SPACE = ("zh", "x", "y", "c")


def swap_core(block):
    return lax.ppermute(block, "c", [(0, 1), (1, 0)])


def pairs(count, first):
    forth = [(i, (i + 1) % count) for i in range(first, count, 2)]
    return forth + [(b, a) for a, b in forth]


def halo_x(block):
    odd = lax.axis_index("x") % 2 == 1
    first, last = block[:, :1], block[:, -1:]
    outer = lax.ppermute(jnp.where(odd, last, first), ("zh", "x"), pairs(8, 1))
    inner = lax.ppermute(jnp.where(odd, first, last), ("zh", "x"), pairs(8, 0))
    lower = jnp.where(odd, inner, outer)
    upper = jnp.where(odd, outer, inner)
    return jnp.concatenate((lower, block, upper), axis=1)


def outer_rim(ext):
    odd = lax.axis_index("c") == 1
    rim = jnp.where(odd, ext[:, :, -1:], ext[:, :, :1])
    return lax.ppermute(rim, SPACE, pairs(64, 1))


def in_order(own, other, axis):
    second = lax.axis_index("c") == 1
    low = jnp.where(second, other, own)
    high = jnp.where(second, own, other)
    return jnp.concatenate((low, high), axis=axis)


def with_rims(pair, rim, rim_other):
    second = lax.axis_index("c") == 1
    low = jnp.where(second, rim_other, rim)
    high = jnp.where(second, rim, rim_other)
    return jnp.concatenate((low, pair, high), axis=2)


def grad_rows():
    n = jnp.arange(C // 2, dtype=jnp.int32)
    xy, zh, r = n // 8, n // 4 % 2, n % 4
    rows = zh * 128 + xy * 8 + lax.axis_index("c") * 4 + r
    return (rows[:, None] == jnp.arange(C, dtype=jnp.int32)[None, :]).astype(BF16)


def weight_rows():
    n = jnp.arange(C, dtype=jnp.int32)
    core, zh, xy, r = n // 128, n // 64 % 2, n // 4 % 16, n % 4
    gc = (lax.axis_index("c") + core) % 2
    rows = zh * 128 + xy * 8 + gc * 4 + r
    return (n[:, None] == rows[None, :]).astype(BF16)


def fill_shifts(src, dst):
    wide = src[...].astype(F32)
    k = lax.broadcasted_iota(jnp.int32, wide.shape, 0) % 16
    n = wide.shape[0]
    dst[0] = jnp.where(k == 0, 0.0, pltpu.roll(wide, 1, 0)).astype(BF16)
    dst[1] = src[...]
    dst[2] = jnp.where(k == 15, 0.0, pltpu.roll(wide, n - 1, 0)).astype(BF16)


def tap_rows(shifts, lo, pitch, size, c):
    pieces = (shifts[c, lo : lo + size], shifts[c, lo + pitch : lo + pitch + size])
    return jnp.concatenate(pieces, axis=0)


NT = (((1,), (1,)), ((), ()))


def wgrad_kernel(groups, rims, vol, cot, perm, out, shifts):
    pitch = vol.shape[0] // 4
    fill_shifts(vol, shifts)
    cot_t = lax.dot_general(perm[...], cot[...], NT, preferred_element_type=F32).astype(BF16)
    for n, (a, b) in enumerate(groups):
        for c in range(3):
            rows = tap_rows(shifts, a * pitch + (b - 1 + rims) * 16, pitch, 256, c)
            lo = (3 * n + c) * C
            sums = jnp.dot(cot_t, rows, preferred_element_type=F32)
            out[:, lo : lo + C] = sums.astype(BF16)


def wgrad(vol, cot, perm, groups, rims):
    vol = vol.reshape(-1, C)
    return pl.pallas_call(
        functools.partial(wgrad_kernel, groups, rims),
        out_shape=jax.ShapeDtypeStruct((128, len(groups) * 3 * C), BF16),
        scratch_shapes=[pltpu.VMEM((3,) + vol.shape, BF16)],
        compiler_params=pltpu.CompilerParams(vmem_limit_bytes=16 << 20),
    )(vol, cot, perm)


def conv_kernel(vol, cot, w0, w1, q, feat, grad, vs, cs):
    fill_shifts(vol, vs)
    fill_shifts(cot, cs)
    acc_f = jnp.zeros((C, C), F32)
    acc_g = jnp.zeros((C, C), F32)
    for g in range(9):
        a, b = g // 3, g % 3
        lo = g * 3 * C
        w = jnp.concatenate((w0[:, lo : lo + 3 * C], w1[:, lo : lo + 3 * C]), axis=0)
        w = jnp.dot(q[...], w, preferred_element_type=F32).astype(BF16)
        at = a * 160 + b * 16
        v = jnp.concatenate([tap_rows(vs, at, 160, 128, c) for c in range(3)], axis=1)
        acc_f += lax.dot_general(v, w, NT, preferred_element_type=F32)
        for c in range(3):
            rows = tap_rows(cs, (2 - a) * 160 + (2 - b) * 16, 160, 128, 2 - c)
            acc_g += jnp.dot(rows, w[:, c * C : c * C + C], preferred_element_type=F32)
    feat[...] = acc_f.astype(BF16)
    grad[...] = acc_g.astype(BF16)


def conv(vol, cot, w0, w1, q):
    out = jax.ShapeDtypeStruct((C, C), BF16)
    return pl.pallas_call(
        conv_kernel,
        out_shape=(out, out),
        scratch_shapes=[pltpu.VMEM((3, 640, C), BF16), pltpu.VMEM((3, 640, C), BF16)],
        compiler_params=pltpu.CompilerParams(vmem_limit_bytes=16 << 20),
    )(vol, cot, w0, w1, q)


def exchange_xy(part):
    return lax.all_to_all(part.reshape(16, 8, -1), ("x", "y"), 0, 0, tiled=True)


def sum_kernel(factor, cols, early, late, out):
    width = 3 * C
    line = {}
    for ref, groups in ((early, EARLY), (late, LATE)):
        for n, g in enumerate(groups):
            part = ref[:, :, n * width : n * width + width].astype(F32)
            line[g] = jnp.sum(part, axis=0) * factor
    line = jnp.concatenate([line[g] for g in sorted(line)], axis=1)
    for d in range(4):
        block = line[:, d * cols : d * cols + cols].astype(out.dtype)
        out[2 * d] = block[:4]
        out[2 * d + 1] = block[4:]


def sum_xy(early, late, factor, rows, cols):
    return pl.pallas_call(
        functools.partial(sum_kernel, factor, cols),
        out_shape=jax.ShapeDtypeStruct((8, rows, cols), BF16),
        compiler_params=pltpu.CompilerParams(vmem_limit_bytes=16 << 20),
    )(early, late)


def ring_z(block, step):
    place = [z % 4 * 2 + z // 4 for z in range(8)]
    route = [(place[z], place[(z + step) % 8]) for z in range(8)]
    return lax.ppermute(block, ("dp", "zh"), route)


def assemble_kernel(z, b0, d1, d2, d3, ux, dx, u3, u2, u1, out, blocks, sems):
    rows = b0.shape[0]
    half = rows // 2
    copies = []
    for rel, ref in enumerate((b0, d1, d2, d3, ux, u3, u2, u1)):
        at = (z[0] + rel) % 8
        if ref is ux:
            copies.append((ux, blocks.at[at, :half]))
            copies.append((dx, blocks.at[at, half:]))
        else:
            copies.append((ref, blocks.at[at]))
    copies = [pltpu.make_async_copy(a, b, sems.at[n]) for n, (a, b) in enumerate(copies)]
    for copy in copies:
        copy.start()
    for copy in copies:
        copy.wait()
    for zh in range(2):
        for r in range(0, rows, 16):
            line = [blocks[zh * 4 + d, r : r + 16] for d in range(4)]
            out[zh * rows + r : zh * rows + r + 16] = jnp.concatenate(line, axis=1)


def gather_z(block):
    rows, cols = block.shape
    up, down = [block], [block]
    for _ in range(3):
        up.append(ring_z(up[-1], 1))
        down.append(ring_z(down[-1], -1))
    ux = ring_z(up[3][: rows // 2], 1)
    dx = ring_z(down[3][rows // 2 :], -1)
    z = (lax.axis_index("zh") * 4 + lax.axis_index("dp")).reshape(1)
    parts = (block, down[1], down[2], down[3], ux, dx, up[3], up[2], up[1])
    whole = pl.BlockSpec(memory_space=pl.ANY)
    return pl.pallas_call(
        assemble_kernel,
        out_shape=jax.ShapeDtypeStruct((2 * rows, 4 * cols), block.dtype),
        in_specs=[pl.BlockSpec(memory_space=pltpu.SMEM)] + [whole] * 9,
        scratch_shapes=[
            pltpu.VMEM((8, rows, cols), block.dtype),
            pltpu.SemaphoreType.DMA((9,)),
        ],
        compiler_params=pltpu.CompilerParams(vmem_limit_bytes=16 << 20),
    )(z, *[pltpu.with_memory_space_constraint(b, pltpu.HBM) for b in parts])


EARLY = ((0, 1), (1, 1), (2, 1))
LATE = ((0, 0), (0, 2), (1, 0), (1, 2), (2, 0), (2, 2))


def step(volumes, weight, cotangent):
    own_cot = cotangent.reshape(C, C)
    rows, cols = weight.shape
    perm = grad_rows()

    ext = halo_x(jnp.stack((volumes[0, 0], cotangent[0, 0])))
    rim = outer_rim(ext)
    pair = in_order(ext, swap_core(ext), 2)
    cots = pair[1, 1:3].reshape(2 * C, C)
    early = wgrad(pair[0], cots, perm, EARLY, 0)
    wide = with_rims(pair, rim, swap_core(rim))
    late = wgrad(wide[0], cots, perm, LATE, 1)
    own = lax.dynamic_slice_in_dim(wide, lax.axis_index("c") * 8, 10, axis=2)
    own = own.reshape(2, 640, C)

    head = 7 * 128
    fold = jnp.pad(weight[:, head:], ((0, 0), (0, 2 * head - cols)))
    fold = jnp.concatenate((weight[:, :head], fold), axis=0)
    w0 = exchange_xy(jnp.broadcast_to(fold, (16, 2 * rows, head)))
    early = exchange_xy(early)
    late = exchange_xy(late)
    w0 = jnp.concatenate((w0[:, :rows], w0[:, rows:, : cols - head]), axis=2)
    w0 = w0.reshape(16 * rows, cols)
    w0 = gather_z(w0)
    w1 = swap_core(w0)

    factor = 1.0 / math.sqrt(own_cot.shape[0] * lax.axis_size(("dp",) + SPACE))
    part = sum_xy(early, late, factor, rows, cols)
    part = lax.all_to_all(part, ("dp", "zh"), 0, 0, tiled=True)
    weight_grad = jnp.sum(part.astype(F32), axis=0)

    features, input_grad = conv(
        own[0], own[1], w0, w1, weight_rows()
    )
    return (features.reshape(volumes.shape), input_grad.reshape(volumes.shape), weight_grad)


def solution(mesh):
    fine = Mesh(mesh.devices.reshape(4, 2, 4, 4, 2), ("dp",) + SPACE)
    blocks = P("dp", SPACE, None, None, None, None)
    return jax.shard_map(
        step,
        mesh=fine,
        in_specs=(blocks, P(SPACE, "dp"), blocks),
        out_specs=(blocks, blocks, P(SPACE, "dp")),
        check_vma=False,
    )
```
